512 devices in a mesh: space: 64 (over x, y, z_lo), mode: 8 (over z_hi, core).
Axes of the slice: x: 4, y: 8, z: 8 (z_hi: 4, z_lo: 2; z = z_hi * 2 + z_lo), core: 2. Of those that a mesh axis runs over, the one named last changes fastest.
Arguments:
- state: float32 [858, 65536], P(None, ('space', 'mode')), may hold values from -6 to 6
- tensor: bfloat16 [64, 286, 858], P('mode'), may hold values from -0.01171875 to 0.01171875
- table: int32 [286, 3], replicated, may hold values from 0 to 10, as said below
- thermal: float32 [3], replicated, may hold values from 0.5 to 2
- output_mode_row: int32 [64], replicated, may hold values from 0 to 857, as said below
Outputs:
- updated: float32 [858, 65536], P(None, ('space', 'mode'))
- collision: float32 [64, 65536], P('mode', 'space')
The draws below stay inside these ranges and needn't reach their ends.
Inputs may be any that keep to these rules, and one draw needn't show every extreme that they name: `table`: each row holds the three indices of one multi-index of total degree at most 10; every such multi-index is in exactly one row. `output_mode_row`: all entries are different.
All inputs are finite; a program needn't handle non-finite values.
Results may differ from the reference program's by a relative error of at most 0.004.
Values may be sent and summed in bfloat16 or wider, within the bound.
A program may use at most 64 MiB of HBM per device.

```python
import math
import jax
import jax.numpy as jnp
import numpy as np
from jax import lax

DEGREE = 10
CLASSES = 3
MODES = 286
OUT = 64
CELLS = 65536


def draw_table(key, part):
    listing = []
    for along_x in range(DEGREE + 1):
        for along_y in range(DEGREE + 1 - along_x):
            for along_z in range(DEGREE + 1 - along_x - along_y):
                listing.append((along_x, along_y, along_z))
    canonical = jnp.asarray(np.array(listing, dtype=np.int32))
    ordering = jax.random.permutation(jax.random.fold_in(key, 7), canonical.shape[0])
    return canonical[ordering].astype(jnp.int32)


def draw_output_mode_row(key, part):
    ordering = jax.random.permutation(jax.random.fold_in(key, 11), CLASSES * MODES)
    return ordering[:OUT].astype(jnp.int32)


def block_scale(own_key, dims, pieces, low, high):
    def one(position, shards_of):
        steps = jax.random.uniform(jax.random.fold_in(jax.random.fold_in(own_key, 6), position), (shards_of,), jnp.float32, low / len(pieces), high / len(pieces))
        return jnp.repeat(jnp.exp(steps), dims[position] // shards_of).reshape((-1,) + (1,) * (len(dims) - position - 1))

    gain = one(*pieces[0])
    for cut in pieces[1:]:
        gain = gain * one(*cut)
    return gain


def noise(key, extent, deviation, most, split=(), kind=jnp.bfloat16):
    drawn = deviation * jax.random.normal(key, extent, jnp.float32)
    if split:
        drawn = drawn * block_scale(key, extent, split, -0.22, 0.18)
    return jnp.clip(drawn, -most, most).astype(kind)


def setup_inputs(seed: int = 0) -> dict:
    splits = jax.random.split(jax.random.key(seed), 6)
    return {
        "state": noise(splits[0], (CLASSES * MODES, CELLS), 1.0, 6.0, ((1, 512),), jnp.float32),
        "tensor": noise(splits[1], (OUT, MODES, CLASSES * MODES), (MODES * CLASSES * MODES) ** -0.5, 0.01171875, ((0, 8),)),
        "table": draw_table(jax.random.fold_in(splits[5], 71), 0),
        "thermal": jnp.clip(jnp.exp(jax.random.uniform(splits[3], (CLASSES,), jnp.float32, math.log(0.5), math.log(2.0))), 0.5, 2.0),
        "output_mode_row": draw_output_mode_row(jax.random.fold_in(splits[5], 71), 0),
    }


wave_bound = 5.2
courant = 0.09
collision_update = 0.1

def advection_matrix(table):
    codes = table[:, 0] * 144 + table[:, 1] * 12 + table[:, 2]
    along = table[:, 0].astype(jnp.float32)
    lower = (codes[None, :] == codes[:, None] - 144).astype(jnp.float32)
    higher = (codes[None, :] == codes[:, None] + 144).astype(jnp.float32)
    return jnp.sqrt(along)[:, None] * lower + jnp.sqrt(along + 1.0)[:, None] * higher

def upwind_transport(extended, state, matrix, thermal):
    blocks = extended.reshape(CLASSES, MODES, -1)
    state_after_collision = jnp.einsum('ab,cbx->cax', matrix, blocks, precision=lax.Precision.HIGHEST)
    speed = thermal[:, None, None]
    flux = 0.5 * speed * (state_after_collision[:, :, :-1] + state_after_collision[:, :, 1:]) - 0.5 * wave_bound * speed * (blocks[:, :, 1:] - blocks[:, :, :-1])
    change = (flux[:, :, 1:] - flux[:, :, :-1]).reshape(CLASSES * MODES, -1)
    return state - courant * change

def reference(state, tensor, table, thermal, output_mode_row):
    coarse = state.astype(jnp.bfloat16)

    def one_output(pair):
        weights, target = pair
        product = jnp.dot(weights, coarse, preferred_element_type=jnp.float32)
        start = (target // MODES * MODES).astype(jnp.int32)
        first = lax.dynamic_slice_in_dim(coarse, start, MODES, 0).astype(jnp.float32)
        return lax.optimization_barrier(jnp.sum(first * product, axis=0))
    collision = lax.map(one_output, (tensor, output_mode_row))
    matrix = advection_matrix(table)
    extended = jnp.concatenate([state[:, -1:], state, state[:, :1]], axis=1)
    advected_state = upwind_transport(extended, state, matrix, thermal)
    updated = advected_state.at[output_mode_row].add(collision_update * collision)
    return (updated, collision)
```

```python
import functools

import jax
import jax.numpy as jnp
from jax import lax
from jax.experimental import pallas as pl
from jax.experimental.pallas import tpu as pltpu
from jax.sharding import PartitionSpec as P

CLASSES = 3
MODES = 286
ROWS = CLASSES * MODES
PAD = 864
HALF = 432
OWN = 8
TILE_I = 26
TILES_I = MODES // TILE_I

wave_bound = 5.2
courant = 0.09
collision_update = 0.1

MESH = pl.DeviceIdType.MESH


def kernel(
    spaces,
    state_hbm,
    tensor_hbm,
    table_hbm,
    thermal_hbm,
    target_hbm,
    updated_ref,
    collision_ref,
    state,
    tensor,
    table,
    thermal,
    target,
    slab,
    first,
    terms_out,
    terms,
    edge_out,
    edge_in,
    matrix,
    delta,
    base,
    placing,
    load_sem,
    z_send,
    z_recv,
    c_send,
    c_recv,
    t_send,
    t_recv,
    e_send,
    e_recv,
):
    space = lax.axis_index("space")
    me = lax.axis_index("mode")
    q, c = me // 2, me % 2
    partner = me + 1 - 2 * c
    right_q, left_q, far_q = (q + 1) % 4, (q + 3) % 4, (q + 2) % 4
    right, left, far = 2 * right_q + c, 2 * left_q + c, 2 * far_q + c

    after = me + 1
    before = me + 7
    after_space = (space + after // 8) % spaces
    before_space = (space + spaces - 1 + before // 8) % spaces
    after_id = {"space": after_space, "mode": after % 8}
    before_id = {"space": before_space, "mode": before % 8}

    barrier = pltpu.get_barrier_semaphore()
    for step in range(1, 8):
        pl.semaphore_signal(
            barrier, inc=1, device_id={"mode": (me + step) % 8}, device_id_type=MESH
        )
    pl.semaphore_signal(barrier, inc=1, device_id=after_id, device_id_type=MESH)
    pl.semaphore_signal(barrier, inc=1, device_id=before_id, device_id_type=MESH)

    def load(source, dest, sem):
        copy = pltpu.make_async_copy(source, dest, load_sem.at[sem])
        copy.start()
        return copy

    state_load = load(state_hbm, state.at[pl.ds(0, ROWS)], 0)
    tensor_load = load(tensor_hbm, tensor, 1)
    table_load = load(table_hbm, table, 2)
    thermal_load = load(thermal_hbm, thermal, 3)
    target_load = load(target_hbm, target, 4)

    def remote(source, dest, send, recv, device):
        return pltpu.make_async_remote_copy(
            src_ref=source,
            dst_ref=dest,
            send_sem=send,
            recv_sem=recv,
            device_id=device,
            device_id_type=MESH,
        )

    def half(slot, h):
        return slab.at[slot, pl.ds(h * HALF, HALF)]

    def over_z(slot, h, i, device):
        return remote(half(slot, h), half(slot, h), z_send.at[i], z_recv.at[i], {"mode": device})

    def over_chip(slot, h, i):
        return remote(half(slot, h), half(slot, h), c_send.at[i], c_recv.at[i], {"mode": partner})

    state_load.wait()
    state[pl.ds(ROWS, 896 - ROWS), :] = jnp.zeros((896 - ROWS, 128), jnp.float32)
    slab[me] = state[pl.ds(0, PAD), :].astype(jnp.bfloat16)
    pl.semaphore_wait(barrier, 9)

    sends = [
        over_z(me, 0, 0, right),
        over_z(me, 1, 3, left),
        over_z(me, 1, 1, right),
        over_z(me, 0, 4, left),
        over_chip(me, 0, 0),
        over_chip(me, 1, 1),
    ]
    for copy in sends:
        copy.start()

    edge_out[...] = jnp.zeros_like(edge_out)
    for t in range(7):
        turned = jnp.transpose(state[pl.ds(128 * t, 128), :])
        edge_out[0, pl.ds(t, 1), :] = turned[0:1, :]
        edge_out[1, pl.ds(t, 1), :] = turned[127:128, :]
    edges = [
        remote(edge_out.at[0], edge_in.at[1], e_send.at[0], e_recv.at[0], before_id),
        remote(edge_out.at[1], edge_in.at[0], e_send.at[1], e_recv.at[1], after_id),
    ]
    for copy in edges:
        copy.start()

    table_load.wait()
    thermal_load.wait()
    target_load.wait()
    along = table[0:1, :]
    codes = along * 144 + table[1:2, :] * 12 + table[2:3, :]
    spread = jnp.broadcast_to(
        jnp.concatenate([codes.astype(jnp.float32), jnp.zeros((1, 384 - MODES), jnp.float32)], axis=1),
        (128, 384),
    )
    code_column = jnp.transpose(spread)[:MODES, 0:1]
    n = along.astype(jnp.float32)
    gap = code_column - codes.astype(jnp.float32)
    matrix[...] = jnp.where(gap == 144.0, jnp.sqrt(n + 1.0), 0.0) + jnp.where(
        gap == -144.0, jnp.sqrt(n), 0.0
    )
    row_index = lax.broadcasted_iota(jnp.int32, (ROWS, 64), 0)
    placing[...] = jnp.where(row_index == target[...], 1.0, 0.0).astype(jnp.bfloat16)

    spot = lax.broadcasted_iota(jnp.int32, (OWN, 64), 1) - lax.broadcasted_iota(
        jnp.int32, (OWN, 64), 0
    )
    own_target = jnp.sum(
        jnp.where(spot == me * OWN, target[...].astype(jnp.float32), 0.0), axis=1, keepdims=True
    )
    wide = jnp.broadcast_to(own_target, (OWN, 256))
    in_first = wide < float(MODES)
    in_second = wide < float(2 * MODES)

    def collide(chip):
        rhs = jnp.concatenate([slab[2 * chip], slab[2 * chip + 1]], axis=1)[:ROWS, :]
        first[...] = rhs.astype(jnp.float32)

        def tile(k, acc):
            lhs = tensor[pl.ds(pl.multiple_of(k * (TILE_I * OWN), 8), TILE_I * OWN), :]
            product = jnp.dot(lhs, rhs, preferred_element_type=jnp.float32)
            for j in range(TILE_I):
                i = k * TILE_I + j
                rows = [
                    jnp.broadcast_to(first[pl.ds(i + MODES * d, 1), :], (OWN, 256))
                    for d in range(CLASSES)
                ]
                chosen = jnp.where(in_first, rows[0], jnp.where(in_second, rows[1], rows[2]))
                acc = acc + chosen * product[OWN * j : OWN * (j + 1), :]
            return acc

        total = lax.fori_loop(0, TILES_I, tile, jnp.zeros((OWN, 256), jnp.float32))
        terms_out[2 * chip] = total[:, :128]
        terms_out[2 * chip + 1] = total[:, 128:]

    def give(slot):
        return remote(
            terms_out.at[slot], terms.at[me], t_send.at[slot], t_recv.at[me], {"mode": slot}
        )

    tensor_load.wait()
    over_chip(partner, 0, 0).wait_recv()
    over_chip(partner, 1, 1).wait_recv()
    collide(q)
    terms[me] = terms_out[me]
    give(partner).start()

    over_z(left, 0, 0, right).wait_recv()
    passed = [over_z(left, 0, 2, right), over_chip(left, 0, 2)]
    for copy in passed:
        copy.start()
    over_z(right, 1, 3, left).wait_recv()
    more = [over_z(right, 1, 5, left), over_chip(right, 1, 3)]
    for copy in more:
        copy.start()
    passed += more

    edges[0].wait_recv()
    edges[1].wait_recv()
    turned = jnp.transpose(
        jnp.concatenate(
            [edge_in[0], edge_in[1], jnp.zeros((112, 128), jnp.float32)], axis=0
        )
    )
    lane = lax.broadcasted_iota(jnp.int32, (128, 128), 1)
    speed = [thermal[0:1, d : d + 1] for d in range(CLASSES)]
    for t in range(7):
        x = state[pl.ds(128 * t, 128), :]
        lower = jnp.where(lane == 0, turned[:, t : t + 1], pltpu.roll(x, 1, 1))
        upper = jnp.where(lane == 127, turned[:, 8 + t : 9 + t], pltpu.roll(x, 127, 1))
        row = lax.broadcasted_iota(jnp.int32, (128, 128), 0) + 128 * t
        scale = jnp.where(row < MODES, speed[0], jnp.where(row < 2 * MODES, speed[1], speed[2]))
        delta[pl.ds(128 * t, 128), :] = (0.5 * courant) * scale * (upper - lower)
        base[pl.ds(128 * t, 128), :] = x + (0.5 * courant * wave_bound) * scale * (
            (upper - x) - (x - lower)
        )
    for d in range(CLASSES):
        rows = pl.ds(MODES * d, MODES)
        base[rows, :] = base[rows, :] - jnp.dot(
            matrix[...],
            delta[rows, :],
            precision=lax.Precision.HIGHEST,
            preferred_element_type=jnp.float32,
        )

    over_z(left, 1, 1, right).wait_recv()
    over_z(right, 0, 4, left).wait_recv()
    more = [over_chip(left, 1, 4), over_chip(right, 0, 5)]
    for copy in more:
        copy.start()
    passed += more
    left_other, right_other, far_other = (2 * v + 1 - c for v in (left_q, right_q, far_q))
    over_chip(left_other, 0, 2).wait_recv()
    over_chip(left_other, 1, 4).wait_recv()
    collide(left_q)
    give(left).start()
    give(left_other).start()
    over_chip(right_other, 1, 3).wait_recv()
    over_chip(right_other, 0, 5).wait_recv()
    collide(right_q)
    give(right).start()
    give(right_other).start()

    over_z(far, 0, 2, right).wait_recv()
    over_z(far, 1, 5, left).wait_recv()
    more = [over_chip(far, 0, 6), over_chip(far, 1, 7)]
    for copy in more:
        copy.start()
    passed += more
    over_chip(far_other, 0, 6).wait_recv()
    over_chip(far_other, 1, 7).wait_recv()
    collide(far_q)
    give(far).start()
    give(far_other).start()
    for slot in range(8):
        collision_ref[:, 128 * slot : 128 * (slot + 1)] = terms_out[slot]

    others = (partner, left, left_other, right, right_other, far, far_other)
    for other in others:
        remote(
            terms_out.at[other], terms.at[other], t_send.at[other], t_recv.at[other], {"mode": other}
        ).wait_recv()
    scaled = collision_update * terms[...].reshape(64, 128)
    high = scaled.astype(jnp.bfloat16)
    low = (scaled - high.astype(jnp.float32)).astype(jnp.bfloat16)
    updated_ref[...] = (
        base[pl.ds(0, ROWS), :]
        + jnp.dot(placing[...], high, preferred_element_type=jnp.float32)
        + jnp.dot(placing[...], low, preferred_element_type=jnp.float32)
    )
    for copy in sends + passed + edges:
        copy.wait_send()
    for other in others:
        give(other).wait_send()


def shards(spaces, state, tensor, table, thermal, output_mode_row):
    f32, bf16 = jnp.float32, jnp.bfloat16
    flat = jnp.transpose(tensor, (1, 0, 2)).reshape(MODES * OWN, ROWS)
    anywhere = pl.BlockSpec(memory_space=pl.ANY)
    return pl.pallas_call(
        functools.partial(kernel, spaces),
        out_shape=(
            jax.ShapeDtypeStruct((ROWS, 128), f32),
            jax.ShapeDtypeStruct((OWN, 1024), f32),
        ),
        in_specs=[anywhere] * 5,
        out_specs=(pl.BlockSpec(memory_space=pltpu.VMEM),) * 2,
        scratch_shapes=[
            pltpu.VMEM((896, 128), f32),
            pltpu.VMEM((MODES * OWN, ROWS), bf16),
            pltpu.VMEM((3, MODES), jnp.int32),
            pltpu.VMEM((1, CLASSES), f32),
            pltpu.VMEM((1, 64), jnp.int32),
            pltpu.VMEM((8, PAD, 128), bf16),
            pltpu.VMEM((ROWS, 256), f32),
            pltpu.VMEM((8, OWN, 128), f32),
            pltpu.VMEM((8, OWN, 128), f32),
            pltpu.VMEM((2, 8, 128), f32),
            pltpu.VMEM((2, 8, 128), f32),
            pltpu.VMEM((MODES, MODES), f32),
            pltpu.VMEM((896, 128), f32),
            pltpu.VMEM((896, 128), f32),
            pltpu.VMEM((ROWS, 64), bf16),
            pltpu.SemaphoreType.DMA((5,)),
            pltpu.SemaphoreType.DMA((6,)),
            pltpu.SemaphoreType.DMA((6,)),
            pltpu.SemaphoreType.DMA((8,)),
            pltpu.SemaphoreType.DMA((8,)),
            pltpu.SemaphoreType.DMA((8,)),
            pltpu.SemaphoreType.DMA((8,)),
            pltpu.SemaphoreType.DMA((2,)),
            pltpu.SemaphoreType.DMA((2,)),
        ],
        compiler_params=pltpu.CompilerParams(collective_id=0, has_side_effects=True),
    )(state, flat, table.T, thermal.reshape(1, CLASSES), output_mode_row.reshape(1, 64))


def solution(mesh):
    in_specs = (P(None, ("space", "mode")), P("mode", None, None), P(), P(), P())
    out_specs = (P(None, ("space", "mode")), P("mode", "space"))
    return jax.shard_map(
        functools.partial(shards, mesh.shape["space"]),
        mesh=mesh,
        in_specs=in_specs,
        out_specs=out_specs,
        check_vma=False,
    )
```

```python
import functools

import jax
import jax.numpy as jnp
from jax import lax
from jax.experimental import pallas as pl
from jax.experimental.pallas import tpu as pltpu
from jax.sharding import PartitionSpec as P

CLASSES = 3
MODES = 286
ROWS = CLASSES * MODES
PAD = 864
HALF = 432
OWN = 8

wave_bound = 5.2
courant = 0.09
collision_update = 0.1

MESH = pl.DeviceIdType.MESH


def kernel(
    spaces,
    state_hbm,
    tensor_hbm,
    table_hbm,
    thermal_hbm,
    target_hbm,
    updated,
    terms_out,
    state,
    tensor,
    table,
    thermal,
    target,
    slab,
    first,
    terms,
    edge_out,
    edge_in,
    matrix,
    delta,
    base,
    placing,
    load_sem,
    z_send,
    z_recv,
    c_send,
    c_recv,
    t_send,
    t_recv,
    e_send,
    e_recv,
):
    space = lax.axis_index("space")
    me = lax.axis_index("mode")
    q, c = me // 2, me % 2
    partner = me + 1 - 2 * c
    right_q, left_q, far_q = (q + 1) % 4, (q + 3) % 4, (q + 2) % 4
    right, left, far = 2 * right_q + c, 2 * left_q + c, 2 * far_q + c

    after = me + 1
    before = me + 7
    after_space = (space + after // 8) % spaces
    before_space = (space + spaces - 1 + before // 8) % spaces
    after_id = {"space": after_space, "mode": after % 8}
    before_id = {"space": before_space, "mode": before % 8}

    sideways_id = {
        "space": jnp.where(c == 0, before_id["space"], after_id["space"]),
        "mode": jnp.where(c == 0, before_id["mode"], after_id["mode"]),
    }

    barrier = pltpu.get_barrier_semaphore()
    for device in ({"mode": right}, {"mode": left}, {"mode": partner}, sideways_id):
        pl.semaphore_signal(barrier, inc=1, device_id=device, device_id_type=MESH)

    def load(source, dest, sem):
        copy = pltpu.make_async_copy(source, dest, load_sem.at[sem])
        copy.start()
        return copy

    state_load = load(state_hbm, state.at[pl.ds(0, ROWS)], 0)
    table_load = load(table_hbm, table, 2)
    thermal_load = load(thermal_hbm, thermal, 3)
    target_load = load(target_hbm, target, 4)

    def remote(source, dest, send, recv, device):
        return pltpu.make_async_remote_copy(
            src_ref=source,
            dst_ref=dest,
            send_sem=send,
            recv_sem=recv,
            device_id=device,
            device_id_type=MESH,
        )

    def half(slot, h):
        return slab.at[slot, pl.ds(pl.multiple_of(h * HALF, 16), HALF)]

    def over_z(slot, h, i, device):
        return remote(half(slot, h), half(slot, h), z_send.at[i], z_recv.at[i], {"mode": device})

    def over_chip(slot, h, i):
        return remote(half(slot, h), half(slot, h), c_send.at[i], c_recv.at[i], {"mode": partner})

    state_load.wait()
    tensor_load = load(tensor_hbm, tensor, 1)
    state[pl.ds(ROWS, 896 - ROWS), :] = jnp.zeros((896 - ROWS, 128), jnp.float32)
    slab[me] = state[pl.ds(0, PAD), :].astype(jnp.bfloat16)

    edge_out[...] = jnp.zeros_like(edge_out)
    for t in range(7):
        turned = jnp.transpose(state[pl.ds(128 * t, 128), :])
        edge_out[0, pl.ds(t, 1), :] = turned[0:1, :]
        edge_out[1, pl.ds(t, 1), :] = turned[127:128, :]
    edges = [
        remote(edge_out.at[0], edge_in.at[1], e_send.at[0], e_recv.at[0], before_id),
        remote(edge_out.at[1], edge_in.at[0], e_send.at[1], e_recv.at[1], after_id),
    ]
    pl.semaphore_wait(barrier, 4)

    own = [
        over_z(me, 0, 0, right),
        over_z(me, 1, 1, left),
        over_z(me, 1, 2, right),
        over_z(me, 0, 3, left),
        over_chip(me, 0, 0),
        over_chip(me, 1, 1),
    ]
    for copy in edges + own:
        copy.start()

    table_load.wait()
    thermal_load.wait()
    target_load.wait()
    along = table[0:1, :]
    codes = along * 144 + table[1:2, :] * 12 + table[2:3, :]
    spread = jnp.broadcast_to(
        jnp.concatenate([codes.astype(jnp.float32), jnp.zeros((1, 384 - MODES), jnp.float32)], axis=1),
        (128, 384),
    )
    code_column = jnp.transpose(spread)[:MODES, 0:1]
    n = along.astype(jnp.float32)
    gap = code_column - codes.astype(jnp.float32)
    matrix[...] = jnp.where(gap == 144.0, jnp.sqrt(n + 1.0), 0.0) + jnp.where(
        gap == -144.0, jnp.sqrt(n), 0.0
    )
    row_index = lax.broadcasted_iota(jnp.int32, (ROWS, 64), 0)
    placing[...] = jnp.where(row_index == target[...], 1.0, 0.0).astype(jnp.bfloat16)

    spot = lax.broadcasted_iota(jnp.int32, (OWN, 64), 1) - lax.broadcasted_iota(
        jnp.int32, (OWN, 64), 0
    )
    own_target = jnp.sum(
        jnp.where(spot == me * OWN, target[...].astype(jnp.float32), 0.0), axis=1, keepdims=True
    )
    wide = jnp.broadcast_to(own_target, (OWN, 256))
    in_first = wide < float(MODES)
    in_second = wide < float(2 * MODES)

    def transport():
        edges[0].wait_recv()
        edges[1].wait_recv()
        turned = jnp.transpose(
            jnp.concatenate(
                [edge_in[0], edge_in[1], jnp.zeros((112, 128), jnp.float32)], axis=0
            )
        )
        lane = lax.broadcasted_iota(jnp.int32, (128, 128), 1)
        speed = [thermal[0:1, d : d + 1] for d in range(CLASSES)]
        for t in range(7):
            x = state[pl.ds(128 * t, 128), :]
            lower = jnp.where(lane == 0, turned[:, t : t + 1], pltpu.roll(x, 1, 1))
            upper = jnp.where(lane == 127, turned[:, 8 + t : 9 + t], pltpu.roll(x, 127, 1))
            row = lax.broadcasted_iota(jnp.int32, (128, 128), 0) + 128 * t
            scale = jnp.where(
                row < MODES, speed[0], jnp.where(row < 2 * MODES, speed[1], speed[2])
            )
            delta[pl.ds(128 * t, 128), :] = (0.5 * courant) * scale * (upper - lower)
            base[pl.ds(128 * t, 128), :] = x + (0.5 * courant * wave_bound) * scale * (
                (upper - x) - (x - lower)
            )
        for d in range(CLASSES):
            rows = pl.ds(MODES * d, MODES)
            base[rows, :] = base[rows, :] - jnp.dot(
                matrix[...],
                delta[rows, :],
                precision=lax.Precision.HIGHEST,
                preferred_element_type=jnp.float32,
            )

    def give(slot):
        return remote(
            terms_out.at[slot], terms.at[me], t_send.at[slot], t_recv.at[me], {"mode": slot}
        )

    def take(other):
        return remote(
            terms_out.at[other], terms.at[other], t_send.at[other], t_recv.at[other], {"mode": other}
        )

    near = jnp.where((q == 0) | (q == 3), 1, 0)
    sides = (near, 1 - near)

    def side_chip(side):
        return jnp.where(side == 0, left_q, right_q)

    def pass_early(side):
        slot, back = 2 * side_chip(side) + c, 2 * side_chip(1 - side) + c
        over_z(slot, side, side, back).wait_recv()
        over_z(slot, side, 4 + side, back).start()
        over_chip(slot, side, 2 + side).start()

    def pass_late(side):
        slot, back = 2 * side_chip(side) + c, 2 * side_chip(1 - side) + c
        over_z(slot, 1 - side, 2 + side, back).wait_recv()
        over_chip(slot, 1 - side, 4 + side).start()

    def await_partner(side):
        slot = 2 * side_chip(side) + 1 - c
        over_chip(slot, side, 2 + side).wait_recv()
        over_chip(slot, 1 - side, 4 + side).wait_recv()

    def step(k, carry):
        @pl.when(k == 0)
        def _():
            tensor_load.wait()
            over_chip(partner, 0, 0).wait_recv()
            over_chip(partner, 1, 1).wait_recv()

        @pl.when(k == 1)
        def _():
            pass_early(0)
            pass_early(1)
            transport()
            pass_late(sides[0])
            pass_late(sides[1])
            await_partner(sides[0])

        @pl.when(k == 2)
        def _():
            await_partner(sides[1])

        @pl.when(k == 3)
        def _():
            for side in range(2):
                over_z(far, side, 4 + side, right).wait_recv()
                over_chip(far, side, 6 + side).start()
            for side in range(2):
                over_chip(2 * far_q + 1 - c, side, 6 + side).wait_recv()

        chip = jnp.where(
            k == 0, q, jnp.where(k == 1, side_chip(near), jnp.where(k == 2, side_chip(1 - near), far_q))
        )
        rhs = jnp.concatenate([slab[2 * chip], slab[2 * chip + 1]], axis=1)[:ROWS, :]
        first[...] = rhs.astype(jnp.float32)
        product = jnp.dot(tensor[...], rhs, preferred_element_type=jnp.float32)
        total = [jnp.zeros((OWN, 256), jnp.float32)] * 4
        for i in range(MODES):
            rows = [
                jnp.broadcast_to(first[pl.ds(i + MODES * d, 1), :], (OWN, 256))
                for d in range(CLASSES)
            ]
            chosen = jnp.where(in_first, rows[0], jnp.where(in_second, rows[1], rows[2]))
            total[i % 4] += chosen * product[OWN * i : OWN * (i + 1), :]
        total = (total[0] + total[1]) + (total[2] + total[3])
        terms_out[2 * chip] = total[:, :128]
        terms_out[2 * chip + 1] = total[:, 128:]
        give(2 * chip + 1 - c).start()

        @pl.when(k == 0)
        def _():
            terms[me] = terms_out[me]

        @pl.when(k > 0)
        def _():
            give(2 * chip + c).start()

        return carry

    lax.fori_loop(0, 4, step, 0)

    others = [(me + v) % 8 for v in range(1, 8)]
    for other in others:
        take(other).wait_recv()
    scaled = collision_update * terms[...].reshape(64, 128)
    high = scaled.astype(jnp.bfloat16)
    low = (scaled - high.astype(jnp.float32)).astype(jnp.bfloat16)
    updated[...] = (
        base[pl.ds(0, ROWS), :]
        + jnp.dot(placing[...], high, preferred_element_type=jnp.float32)
        + jnp.dot(placing[...], low, preferred_element_type=jnp.float32)
    )
    for copy in own + edges:
        copy.wait_send()
    for side in range(2):
        over_z(me, side, 4 + side, right).wait_send()
        for i in (2, 4, 6):
            over_chip(me, side, i + side).wait_send()
    for other in others:
        give(other).wait_send()


def finish(updated, terms, updated_hbm, collision_hbm, sems):
    copies = [pltpu.make_async_copy(updated, updated_hbm, sems.at[8])]
    for slot in range(8):
        copies.append(
            pltpu.make_async_copy(
                terms.at[slot], collision_hbm.at[:, pl.ds(128 * slot, 128)], sems.at[slot]
            )
        )
    for copy in copies:
        copy.start()
    for copy in copies:
        copy.wait()


def shards(spaces, state, tensor, table, thermal, output_mode_row):
    f32, bf16 = jnp.float32, jnp.bfloat16
    flat = jnp.transpose(tensor, (1, 0, 2)).reshape(MODES * OWN, ROWS)
    anywhere = pl.BlockSpec(memory_space=pl.ANY)
    updated, terms = pl.pallas_call(
        functools.partial(kernel, spaces),
        out_shape=(pltpu.VMEM((ROWS, 128), f32), pltpu.VMEM((8, OWN, 128), f32)),
        in_specs=[anywhere] * 5,
        scratch_shapes=[
            pltpu.VMEM((896, 128), f32),
            pltpu.VMEM((MODES * OWN, ROWS), bf16),
            pltpu.VMEM((3, MODES), jnp.int32),
            pltpu.VMEM((1, CLASSES), f32),
            pltpu.VMEM((1, 64), jnp.int32),
            pltpu.VMEM((8, PAD, 128), bf16),
            pltpu.VMEM((ROWS, 256), f32),
            pltpu.VMEM((8, OWN, 128), f32),
            pltpu.VMEM((2, 8, 128), f32),
            pltpu.VMEM((2, 8, 128), f32),
            pltpu.VMEM((MODES, MODES), f32),
            pltpu.VMEM((896, 128), f32),
            pltpu.VMEM((896, 128), f32),
            pltpu.VMEM((ROWS, 64), bf16),
            pltpu.SemaphoreType.DMA((5,)),
            pltpu.SemaphoreType.DMA((6,)),
            pltpu.SemaphoreType.DMA((6,)),
            pltpu.SemaphoreType.DMA((8,)),
            pltpu.SemaphoreType.DMA((8,)),
            pltpu.SemaphoreType.DMA((8,)),
            pltpu.SemaphoreType.DMA((8,)),
            pltpu.SemaphoreType.DMA((2,)),
            pltpu.SemaphoreType.DMA((2,)),
        ],
        compiler_params=pltpu.CompilerParams(collective_id=0, has_side_effects=True),
    )(state, flat, table.T, thermal.reshape(1, CLASSES), output_mode_row.reshape(1, 64))
    return pl.pallas_call(
        finish,
        out_shape=(
            jax.ShapeDtypeStruct((ROWS, 128), f32),
            jax.ShapeDtypeStruct((OWN, 1024), f32),
        ),
        in_specs=[pl.BlockSpec(memory_space=pltpu.VMEM)] * 2,
        out_specs=(anywhere,) * 2,
        scratch_shapes=[pltpu.SemaphoreType.DMA((9,))],
    )(pltpu.with_memory_space_constraint(updated, pltpu.VMEM), pltpu.with_memory_space_constraint(terms, pltpu.VMEM))


def solution(mesh):
    in_specs = (P(None, ("space", "mode")), P("mode", None, None), P(), P(), P())
    out_specs = (P(None, ("space", "mode")), P("mode", "space"))
    return jax.shard_map(
        functools.partial(shards, mesh.shape["space"]),
        mesh=mesh,
        in_specs=in_specs,
        out_specs=out_specs,
        check_vma=False,
    )
```

```python
import functools

import jax
import jax.numpy as jnp
from jax import lax
from jax.experimental import pallas as pl
from jax.experimental.pallas import tpu as pltpu
from jax.sharding import PartitionSpec as P

CLASSES = 3
MODES = 286
ROWS = CLASSES * MODES
PAD = 864
HALF = 432
OWN = 8

wave_bound = 5.2
courant = 0.09
collision_update = 0.1

MESH = pl.DeviceIdType.MESH


def kernel(
    spaces,
    state_hbm,
    tensor_hbm,
    table_hbm,
    thermal_hbm,
    target_hbm,
    updated,
    terms_out,
    state,
    tensor,
    table,
    thermal,
    target,
    slab,
    first,
    terms,
    edge_out,
    edge_in,
    matrix,
    delta,
    base,
    placing,
    load_sem,
    z_send,
    z_recv,
    c_send,
    c_recv,
    t_send,
    t_recv,
    e_send,
    e_recv,
):
    space = lax.axis_index("space")
    me = lax.axis_index("mode")
    q, c = me // 2, me % 2
    partner = me + 1 - 2 * c
    right_q, left_q, far_q = (q + 1) % 4, (q + 3) % 4, (q + 2) % 4
    right, left, far = 2 * right_q + c, 2 * left_q + c, 2 * far_q + c

    after = me + 1
    before = me + 7
    after_space = (space + after // 8) % spaces
    before_space = (space + spaces - 1 + before // 8) % spaces
    after_id = {"space": after_space, "mode": after % 8}
    before_id = {"space": before_space, "mode": before % 8}

    sideways_id = {
        "space": jnp.where(c == 0, before_id["space"], after_id["space"]),
        "mode": jnp.where(c == 0, before_id["mode"], after_id["mode"]),
    }

    barrier = pltpu.get_barrier_semaphore()
    for device in ({"mode": right}, {"mode": left}, {"mode": partner}, sideways_id):
        pl.semaphore_signal(barrier, inc=1, device_id=device, device_id_type=MESH)

    def load(source, dest, sem):
        copy = pltpu.make_async_copy(source, dest, load_sem.at[sem])
        copy.start()
        return copy

    state_load = load(state_hbm, state.at[pl.ds(0, ROWS)], 0)
    table_load = load(table_hbm, table, 2)
    thermal_load = load(thermal_hbm, thermal, 3)
    target_load = load(target_hbm, target, 4)

    def remote(source, dest, send, recv, device):
        return pltpu.make_async_remote_copy(
            src_ref=source,
            dst_ref=dest,
            send_sem=send,
            recv_sem=recv,
            device_id=device,
            device_id_type=MESH,
        )

    def half(slot, h):
        return slab.at[slot, pl.ds(pl.multiple_of(h * HALF, 16), HALF)]

    def over_z(slot, h, i, device):
        return remote(half(slot, h), half(slot, h), z_send.at[i], z_recv.at[i], {"mode": device})

    def over_chip(slot, h, i):
        return remote(half(slot, h), half(slot, h), c_send.at[i], c_recv.at[i], {"mode": partner})

    state_load.wait()
    tensor_load = load(tensor_hbm, tensor, 1)
    state[pl.ds(ROWS, 896 - ROWS), :] = jnp.zeros((896 - ROWS, 128), jnp.float32)
    slab[me] = state[pl.ds(0, PAD), :].astype(jnp.bfloat16)

    edge_out[...] = jnp.zeros_like(edge_out)
    for t in range(7):
        turned = jnp.transpose(state[pl.ds(128 * t, 128), :])
        edge_out[0, pl.ds(t, 1), :] = turned[0:1, :]
        edge_out[1, pl.ds(t, 1), :] = turned[127:128, :]
    edges = [
        remote(edge_out.at[0], edge_in.at[1], e_send.at[0], e_recv.at[0], before_id),
        remote(edge_out.at[1], edge_in.at[0], e_send.at[1], e_recv.at[1], after_id),
    ]
    pl.semaphore_wait(barrier, 4)

    own = [
        over_z(me, 0, 0, right),
        over_z(me, 1, 1, left),
        over_z(me, 1, 2, right),
        over_z(me, 0, 3, left),
        over_chip(me, 0, 0),
        over_chip(me, 1, 1),
    ]
    for copy in edges + own:
        copy.start()

    table_load.wait()
    thermal_load.wait()
    target_load.wait()
    along = table[0:1, :]
    codes = along * 144 + table[1:2, :] * 12 + table[2:3, :]
    spread = jnp.broadcast_to(
        jnp.concatenate([codes.astype(jnp.float32), jnp.zeros((1, 384 - MODES), jnp.float32)], axis=1),
        (128, 384),
    )
    code_column = jnp.transpose(spread)[:MODES, 0:1]
    n = along.astype(jnp.float32)
    gap = code_column - codes.astype(jnp.float32)
    matrix[...] = jnp.where(gap == 144.0, jnp.sqrt(n + 1.0), 0.0) + jnp.where(
        gap == -144.0, jnp.sqrt(n), 0.0
    )
    row_index = lax.broadcasted_iota(jnp.int32, (ROWS, 128), 0)
    twice = jnp.concatenate([target[...], target[...]], axis=1)
    placing[...] = jnp.where(row_index == twice, 1.0, 0.0).astype(jnp.bfloat16)

    spot = lax.broadcasted_iota(jnp.int32, (OWN, 64), 1) - lax.broadcasted_iota(
        jnp.int32, (OWN, 64), 0
    )
    own_target = jnp.sum(
        jnp.where(spot == me * OWN, target[...].astype(jnp.float32), 0.0), axis=1, keepdims=True
    )
    wide = jnp.broadcast_to(own_target, (OWN, 256))
    in_first = wide < float(MODES)
    in_second = wide < float(2 * MODES)

    def transport():
        edges[0].wait_recv()
        edges[1].wait_recv()
        turned = jnp.transpose(
            jnp.concatenate(
                [edge_in[0], edge_in[1], jnp.zeros((112, 128), jnp.float32)], axis=0
            )
        )
        lane = lax.broadcasted_iota(jnp.int32, (128, 128), 1)
        speed = [thermal[0:1, d : d + 1] for d in range(CLASSES)]
        for t in range(7):
            x = state[pl.ds(128 * t, 128), :]
            lower = jnp.where(lane == 0, turned[:, t : t + 1], pltpu.roll(x, 1, 1))
            upper = jnp.where(lane == 127, turned[:, 8 + t : 9 + t], pltpu.roll(x, 127, 1))
            row = lax.broadcasted_iota(jnp.int32, (128, 128), 0) + 128 * t
            scale = jnp.where(
                row < MODES, speed[0], jnp.where(row < 2 * MODES, speed[1], speed[2])
            )
            delta[pl.ds(128 * t, 128), :] = (0.5 * courant) * scale * (upper - lower)
            base[pl.ds(128 * t, 128), :] = x + (0.5 * courant * wave_bound) * scale * (
                (upper - x) - (x - lower)
            )
        for d in range(CLASSES):
            rows = pl.ds(MODES * d, MODES)
            base[rows, :] = base[rows, :] - jnp.dot(
                matrix[...],
                delta[rows, :],
                precision=lax.Precision.HIGHEST,
                preferred_element_type=jnp.float32,
            )

    def give(slot):
        return remote(
            terms_out.at[slot], terms.at[me], t_send.at[slot], t_recv.at[me], {"mode": slot}
        )

    def take(other):
        return remote(
            terms_out.at[other], terms.at[other], t_send.at[other], t_recv.at[other], {"mode": other}
        )

    near = jnp.where((q == 0) | (q == 3), 1, 0)
    sides = (near, 1 - near)

    def side_chip(side):
        return jnp.where(side == 0, left_q, right_q)

    near_q, next_q = side_chip(near), side_chip(1 - near)
    order = (
        q,
        jnp.where(q == 2, far_q, near_q),
        jnp.where(q == 2, near_q, jnp.where(q == 3, far_q, next_q)),
        jnp.where(q < 2, far_q, next_q),
    )

    def pass_early(side):
        slot, back = 2 * side_chip(side) + c, 2 * side_chip(1 - side) + c
        over_z(slot, side, side, back).wait_recv()
        over_z(slot, side, 4 + side, back).start()
        over_chip(slot, side, 2 + side).start()

    def pass_late(side):
        slot, back = 2 * side_chip(side) + c, 2 * side_chip(1 - side) + c
        over_z(slot, 1 - side, 2 + side, back).wait_recv()
        over_chip(slot, 1 - side, 4 + side).start()

    def pass_far():
        for side in range(2):
            over_z(far, side, 4 + side, right).wait_recv()
            over_chip(far, side, 6 + side).start()

    def await_partner(chip):
        slot = 2 * chip + 1 - c
        low = jnp.where(chip == left_q, 2, jnp.where(chip == right_q, 5, 6))
        high = jnp.where(chip == left_q, 4, jnp.where(chip == right_q, 3, 7))
        over_chip(slot, 0, low).wait_recv()
        over_chip(slot, 1, high).wait_recv()

    def step(k, carry):
        chip = jnp.where(k == 0, order[0], jnp.where(k == 1, order[1], jnp.where(k == 2, order[2], order[3])))

        @pl.when(k == 0)
        def _():
            pass_early(0)
            pass_early(1)
            tensor_load.wait()
            over_chip(partner, 0, 0).wait_recv()
            over_chip(partner, 1, 1).wait_recv()

        @pl.when(k == 1)
        def _():
            pass_late(sides[0])
            pass_late(sides[1])

        @pl.when(k == jnp.where(q == 2, 1, 2))
        def _():
            pass_far()

        @pl.when(k > 0)
        def _():
            await_partner(chip)

        rhs = jnp.concatenate([slab[2 * chip], slab[2 * chip + 1]], axis=1)[:ROWS, :]
        first[...] = rhs.astype(jnp.float32)
        product = jnp.dot(tensor[...], rhs, preferred_element_type=jnp.float32)
        total = [jnp.zeros((OWN, 256), jnp.float32)] * 4
        for i in range(MODES):
            rows = [
                jnp.broadcast_to(first[pl.ds(i + MODES * d, 1), :], (OWN, 256))
                for d in range(CLASSES)
            ]
            chosen = jnp.where(in_first, rows[0], jnp.where(in_second, rows[1], rows[2]))
            total[i % 4] += chosen * product[OWN * i : OWN * (i + 1), :]
        total = (total[0] + total[1]) + (total[2] + total[3])
        terms_out[2 * chip] = total[:, :128]
        terms_out[2 * chip + 1] = total[:, 128:]
        give(2 * chip + 1 - c).start()

        @pl.when(k == 0)
        def _():
            terms[me] = terms_out[me]

        @pl.when(k > 0)
        def _():
            give(2 * chip + c).start()

        return carry

    lax.fori_loop(0, 4, step, 0)

    transport()

    others = [(me + v) % 8 for v in range(1, 8)]
    for other in others:
        take(other).wait_recv()
    scaled = collision_update * terms[...].reshape(64, 128)
    high = scaled.astype(jnp.bfloat16)
    low = (scaled - high.astype(jnp.float32)).astype(jnp.bfloat16)
    updated[...] = (
        base[pl.ds(0, ROWS), :]
        + jnp.dot(
            placing[...],
            jnp.concatenate([high, low], axis=0),
            preferred_element_type=jnp.float32,
        )
    )
    for copy in own + edges:
        copy.wait_send()
    for side in range(2):
        over_z(me, side, 4 + side, right).wait_send()
        for i in (2, 4, 6):
            over_chip(me, side, i + side).wait_send()
    for other in others:
        give(other).wait_send()


def finish(updated, terms, updated_hbm, collision_hbm, sems):
    copies = []
    for part in range(4):
        rows = pl.ds(216 * part, min(216, ROWS - 216 * part))
        copies.append(
            pltpu.make_async_copy(updated.at[rows], updated_hbm.at[rows], sems.at[8 + part])
        )
    for slot in range(8):
        copies.append(
            pltpu.make_async_copy(
                terms.at[slot], collision_hbm.at[:, pl.ds(128 * slot, 128)], sems.at[slot]
            )
        )
    for copy in copies:
        copy.start()
    for copy in copies:
        copy.wait()


def shards(spaces, state, tensor, table, thermal, output_mode_row):
    f32, bf16 = jnp.float32, jnp.bfloat16
    flat = jnp.transpose(tensor, (1, 0, 2)).reshape(MODES * OWN, ROWS)
    anywhere = pl.BlockSpec(memory_space=pl.ANY)
    updated, terms = pl.pallas_call(
        functools.partial(kernel, spaces),
        out_shape=(pltpu.VMEM((ROWS, 128), f32), pltpu.VMEM((8, OWN, 128), f32)),
        in_specs=[anywhere] * 5,
        scratch_shapes=[
            pltpu.VMEM((896, 128), f32),
            pltpu.VMEM((MODES * OWN, ROWS), bf16),
            pltpu.VMEM((3, MODES), jnp.int32),
            pltpu.VMEM((1, CLASSES), f32),
            pltpu.VMEM((1, 64), jnp.int32),
            pltpu.VMEM((8, PAD, 128), bf16),
            pltpu.VMEM((ROWS, 256), f32),
            pltpu.VMEM((8, OWN, 128), f32),
            pltpu.VMEM((2, 8, 128), f32),
            pltpu.VMEM((2, 8, 128), f32),
            pltpu.VMEM((MODES, MODES), f32),
            pltpu.VMEM((896, 128), f32),
            pltpu.VMEM((896, 128), f32),
            pltpu.VMEM((ROWS, 128), bf16),
            pltpu.SemaphoreType.DMA((5,)),
            pltpu.SemaphoreType.DMA((6,)),
            pltpu.SemaphoreType.DMA((6,)),
            pltpu.SemaphoreType.DMA((8,)),
            pltpu.SemaphoreType.DMA((8,)),
            pltpu.SemaphoreType.DMA((8,)),
            pltpu.SemaphoreType.DMA((8,)),
            pltpu.SemaphoreType.DMA((2,)),
            pltpu.SemaphoreType.DMA((2,)),
        ],
        compiler_params=pltpu.CompilerParams(collective_id=0, has_side_effects=True),
    )(state, flat, table.T, thermal.reshape(1, CLASSES), output_mode_row.reshape(1, 64))
    return pl.pallas_call(
        finish,
        out_shape=(
            jax.ShapeDtypeStruct((ROWS, 128), f32),
            jax.ShapeDtypeStruct((OWN, 1024), f32),
        ),
        in_specs=[pl.BlockSpec(memory_space=pltpu.VMEM)] * 2,
        out_specs=(anywhere,) * 2,
        scratch_shapes=[pltpu.SemaphoreType.DMA((12,))],
    )(pltpu.with_memory_space_constraint(updated, pltpu.VMEM), pltpu.with_memory_space_constraint(terms, pltpu.VMEM))


def solution(mesh):
    in_specs = (P(None, ("space", "mode")), P("mode", None, None), P(), P(), P())
    out_specs = (P(None, ("space", "mode")), P("mode", "space"))
    return jax.shard_map(
        functools.partial(shards, mesh.shape["space"]),
        mesh=mesh,
        in_specs=in_specs,
        out_specs=out_specs,
        check_vma=False,
    )
```

```python
import functools

import jax
import jax.numpy as jnp
from jax import lax
from jax.experimental import pallas as pl
from jax.experimental.pallas import tpu as pltpu
from jax.sharding import PartitionSpec as P

CLASSES = 3
MODES = 286
ROWS = CLASSES * MODES
PAD = 864
HALF = 432
OWN = 8

wave_bound = 5.2
courant = 0.09
collision_update = 0.1

MESH = pl.DeviceIdType.MESH


def kernel(
    spaces,
    state_hbm,
    tensor_hbm,
    table_hbm,
    thermal_hbm,
    target_hbm,
    updated,
    terms_out,
    state,
    tensor,
    table,
    thermal,
    target,
    slab,
    first,
    terms,
    edge_out,
    edge_in,
    matrix,
    delta,
    base,
    placing,
    load_sem,
    z_send,
    z_recv,
    c_send,
    c_recv,
    t_send,
    t_recv,
    e_send,
    e_recv,
):
    space = lax.axis_index("space")
    me = lax.axis_index("mode")
    q, c = me // 2, me % 2
    partner = me + 1 - 2 * c
    right_q, left_q, far_q = (q + 1) % 4, (q + 3) % 4, (q + 2) % 4
    right, left, far = 2 * right_q + c, 2 * left_q + c, 2 * far_q + c

    after = me + 1
    before = me + 7
    after_space = (space + after // 8) % spaces
    before_space = (space + spaces - 1 + before // 8) % spaces
    after_id = {"space": after_space, "mode": after % 8}
    before_id = {"space": before_space, "mode": before % 8}

    sideways_id = {
        "space": jnp.where(c == 0, before_id["space"], after_id["space"]),
        "mode": jnp.where(c == 0, before_id["mode"], after_id["mode"]),
    }

    barrier = pltpu.get_barrier_semaphore()
    for device in ({"mode": right}, {"mode": left}, {"mode": partner}, sideways_id):
        pl.semaphore_signal(barrier, inc=1, device_id=device, device_id_type=MESH)

    def load(source, dest, sem):
        copy = pltpu.make_async_copy(source, dest, load_sem.at[sem])
        copy.start()
        return copy

    state_loads = []
    for part in range(4):
        rows = pl.ds(216 * part, min(216, ROWS - 216 * part))
        state_loads.append(load(state_hbm.at[rows], state.at[rows], 5 + part))
    table_load = load(table_hbm, table, 2)
    thermal_load = load(thermal_hbm, thermal, 3)
    target_load = load(target_hbm, target, 4)

    def remote(source, dest, send, recv, device):
        return pltpu.make_async_remote_copy(
            src_ref=source,
            dst_ref=dest,
            send_sem=send,
            recv_sem=recv,
            device_id=device,
            device_id_type=MESH,
        )

    def half(slot, h):
        return slab.at[slot, pl.ds(pl.multiple_of(h * HALF, 16), HALF)]

    def over_z(slot, h, i, device):
        return remote(half(slot, h), half(slot, h), z_send.at[i], z_recv.at[i], {"mode": device})

    def over_chip(slot, h, i):
        return remote(half(slot, h), half(slot, h), c_send.at[i], c_recv.at[i], {"mode": partner})

    for copy in state_loads:
        copy.wait()
    tensor_load = load(tensor_hbm, tensor, 1)
    state[pl.ds(ROWS, 896 - ROWS), :] = jnp.zeros((896 - ROWS, 128), jnp.float32)
    slab[me] = state[pl.ds(0, PAD), :].astype(jnp.bfloat16)

    pl.semaphore_wait(barrier, 4)

    own = [
        over_z(me, 0, 0, right),
        over_z(me, 1, 1, left),
        over_z(me, 1, 2, right),
        over_z(me, 0, 3, left),
        over_chip(me, 0, 0),
        over_chip(me, 1, 1),
    ]
    for copy in own:
        copy.start()

    edge_out[...] = jnp.zeros_like(edge_out)
    for t in range(7):
        turned = jnp.transpose(state[pl.ds(128 * t, 128), :])
        edge_out[0, pl.ds(t, 1), :] = turned[0:1, :]
        edge_out[1, pl.ds(t, 1), :] = turned[127:128, :]
    edges = [
        remote(edge_out.at[0], edge_in.at[1], e_send.at[0], e_recv.at[0], before_id),
        remote(edge_out.at[1], edge_in.at[0], e_send.at[1], e_recv.at[1], after_id),
    ]
    for copy in edges:
        copy.start()

    table_load.wait()
    thermal_load.wait()
    target_load.wait()
    along = table[0:1, :]
    codes = along * 144 + table[1:2, :] * 12 + table[2:3, :]
    spread = jnp.broadcast_to(
        jnp.concatenate([codes.astype(jnp.float32), jnp.zeros((1, 384 - MODES), jnp.float32)], axis=1),
        (128, 384),
    )
    code_column = jnp.transpose(spread)[:MODES, 0:1]
    n = along.astype(jnp.float32)
    gap = code_column - codes.astype(jnp.float32)
    matrix[...] = jnp.where(gap == 144.0, jnp.sqrt(n + 1.0), 0.0) + jnp.where(
        gap == -144.0, jnp.sqrt(n), 0.0
    )
    row_index = lax.broadcasted_iota(jnp.int32, (ROWS, 128), 0)
    twice = jnp.concatenate([target[...], target[...]], axis=1)
    placing[...] = jnp.where(row_index == twice, 1.0, 0.0).astype(jnp.bfloat16)

    spot = lax.broadcasted_iota(jnp.int32, (OWN, 64), 1) - lax.broadcasted_iota(
        jnp.int32, (OWN, 64), 0
    )
    own_target = jnp.sum(
        jnp.where(spot == me * OWN, target[...].astype(jnp.float32), 0.0), axis=1, keepdims=True
    )
    wide = jnp.broadcast_to(own_target, (OWN, 256))
    in_first = wide < float(MODES)
    in_second = wide < float(2 * MODES)

    def transport():
        edges[0].wait_recv()
        edges[1].wait_recv()
        turned = jnp.transpose(
            jnp.concatenate(
                [edge_in[0], edge_in[1], jnp.zeros((112, 128), jnp.float32)], axis=0
            )
        )
        lane = lax.broadcasted_iota(jnp.int32, (128, 128), 1)
        speed = [thermal[0:1, d : d + 1] for d in range(CLASSES)]
        for t in range(7):
            x = state[pl.ds(128 * t, 128), :]
            lower = jnp.where(lane == 0, turned[:, t : t + 1], pltpu.roll(x, 1, 1))
            upper = jnp.where(lane == 127, turned[:, 8 + t : 9 + t], pltpu.roll(x, 127, 1))
            row = lax.broadcasted_iota(jnp.int32, (128, 128), 0) + 128 * t
            scale = jnp.where(
                row < MODES, speed[0], jnp.where(row < 2 * MODES, speed[1], speed[2])
            )
            delta[pl.ds(128 * t, 128), :] = (0.5 * courant) * scale * (upper - lower)
            base[pl.ds(128 * t, 128), :] = x + (0.5 * courant * wave_bound) * scale * (
                (upper - x) - (x - lower)
            )
        for d in range(CLASSES):
            rows = pl.ds(MODES * d, MODES)
            base[rows, :] = base[rows, :] - jnp.dot(
                matrix[...],
                delta[rows, :],
                precision=lax.Precision.HIGHEST,
                preferred_element_type=jnp.float32,
            )

    def give(slot):
        return remote(
            terms_out.at[slot], terms.at[me], t_send.at[slot], t_recv.at[me], {"mode": slot}
        )

    def take(other):
        return remote(
            terms_out.at[other], terms.at[other], t_send.at[other], t_recv.at[other], {"mode": other}
        )

    near = jnp.where((q == 0) | (q == 3), 1, 0)
    sides = (near, 1 - near)

    def side_chip(side):
        return jnp.where(side == 0, left_q, right_q)

    near_q, next_q = side_chip(near), side_chip(1 - near)
    order = (
        q,
        jnp.where(q == 2, far_q, near_q),
        jnp.where(q == 2, near_q, jnp.where(q == 3, far_q, next_q)),
        jnp.where(q < 2, far_q, next_q),
    )

    def pass_early(side):
        slot, back = 2 * side_chip(side) + c, 2 * side_chip(1 - side) + c
        over_z(slot, side, side, back).wait_recv()
        over_z(slot, side, 4 + side, back).start()
        over_chip(slot, side, 2 + side).start()

    def pass_late(side):
        slot, back = 2 * side_chip(side) + c, 2 * side_chip(1 - side) + c
        over_z(slot, 1 - side, 2 + side, back).wait_recv()
        over_chip(slot, 1 - side, 4 + side).start()

    def pass_far():
        for side in range(2):
            over_z(far, side, 4 + side, right).wait_recv()
            over_chip(far, side, 6 + side).start()

    def await_partner(chip):
        slot = 2 * chip + 1 - c
        low = jnp.where(chip == left_q, 2, jnp.where(chip == right_q, 5, 6))
        high = jnp.where(chip == left_q, 4, jnp.where(chip == right_q, 3, 7))
        over_chip(slot, 0, low).wait_recv()
        over_chip(slot, 1, high).wait_recv()

    def step(k, carry):
        chip = jnp.where(k == 0, order[0], jnp.where(k == 1, order[1], jnp.where(k == 2, order[2], order[3])))

        @pl.when(k == 0)
        def _():
            pass_early(0)
            pass_early(1)
            tensor_load.wait()
            over_chip(partner, 0, 0).wait_recv()
            over_chip(partner, 1, 1).wait_recv()

        @pl.when(k == 1)
        def _():
            pass_late(sides[0])
            pass_late(sides[1])

        @pl.when(k == jnp.where(q == 2, 1, 2))
        def _():
            pass_far()

        @pl.when(k > 0)
        def _():
            await_partner(chip)

        rhs = jnp.concatenate([slab[2 * chip], slab[2 * chip + 1]], axis=1)[:ROWS, :]
        first[...] = rhs.astype(jnp.float32)
        product = jnp.dot(tensor[...], rhs, preferred_element_type=jnp.float32)
        total = [jnp.zeros((OWN, 256), jnp.float32)] * 4
        for i in range(MODES):
            rows = [
                jnp.broadcast_to(first[pl.ds(i + MODES * d, 1), :], (OWN, 256))
                for d in range(CLASSES)
            ]
            chosen = jnp.where(in_first, rows[0], jnp.where(in_second, rows[1], rows[2]))
            total[i % 4] += chosen * product[OWN * i : OWN * (i + 1), :]
        total = (total[0] + total[1]) + (total[2] + total[3])
        terms_out[2 * chip] = total[:, :128]
        terms_out[2 * chip + 1] = total[:, 128:]
        give(2 * chip + 1 - c).start()

        @pl.when(k == 0)
        def _():
            terms[me] = terms_out[me]

        @pl.when(k > 0)
        def _():
            give(2 * chip + c).start()

        return carry

    lax.fori_loop(0, 4, step, 0)

    transport()

    others = [(me + v) % 8 for v in range(1, 8)]
    for other in others:
        take(other).wait_recv()
    scaled = collision_update * terms[...].reshape(64, 128)
    high = scaled.astype(jnp.bfloat16)
    low = (scaled - high.astype(jnp.float32)).astype(jnp.bfloat16)
    updated[...] = (
        base[pl.ds(0, ROWS), :]
        + jnp.dot(
            placing[...],
            jnp.concatenate([high, low], axis=0),
            preferred_element_type=jnp.float32,
        )
    )
    for copy in own + edges:
        copy.wait_send()
    for side in range(2):
        over_z(me, side, 4 + side, right).wait_send()
        for i in (2, 4, 6):
            over_chip(me, side, i + side).wait_send()
    for other in others:
        give(other).wait_send()


def finish(updated, terms, updated_hbm, collision_hbm, sems):
    copies = []
    for part in range(4):
        rows = pl.ds(216 * part, min(216, ROWS - 216 * part))
        copies.append(
            pltpu.make_async_copy(updated.at[rows], updated_hbm.at[rows], sems.at[8 + part])
        )
    for slot in range(8):
        copies.append(
            pltpu.make_async_copy(
                terms.at[slot], collision_hbm.at[:, pl.ds(128 * slot, 128)], sems.at[slot]
            )
        )
    for copy in copies:
        copy.start()
    for copy in copies:
        copy.wait()


def shards(spaces, state, tensor, table, thermal, output_mode_row):
    f32, bf16 = jnp.float32, jnp.bfloat16
    flat = jnp.transpose(tensor, (1, 0, 2)).reshape(MODES * OWN, ROWS)
    anywhere = pl.BlockSpec(memory_space=pl.ANY)
    updated, terms = pl.pallas_call(
        functools.partial(kernel, spaces),
        out_shape=(pltpu.VMEM((ROWS, 128), f32), pltpu.VMEM((8, OWN, 128), f32)),
        in_specs=[anywhere] * 5,
        scratch_shapes=[
            pltpu.VMEM((896, 128), f32),
            pltpu.VMEM((MODES * OWN, ROWS), bf16),
            pltpu.VMEM((3, MODES), jnp.int32),
            pltpu.VMEM((1, CLASSES), f32),
            pltpu.VMEM((1, 64), jnp.int32),
            pltpu.VMEM((8, PAD, 128), bf16),
            pltpu.VMEM((ROWS, 256), f32),
            pltpu.VMEM((8, OWN, 128), f32),
            pltpu.VMEM((2, 8, 128), f32),
            pltpu.VMEM((2, 8, 128), f32),
            pltpu.VMEM((MODES, MODES), f32),
            pltpu.VMEM((896, 128), f32),
            pltpu.VMEM((896, 128), f32),
            pltpu.VMEM((ROWS, 128), bf16),
            pltpu.SemaphoreType.DMA((9,)),
            pltpu.SemaphoreType.DMA((6,)),
            pltpu.SemaphoreType.DMA((6,)),
            pltpu.SemaphoreType.DMA((8,)),
            pltpu.SemaphoreType.DMA((8,)),
            pltpu.SemaphoreType.DMA((8,)),
            pltpu.SemaphoreType.DMA((8,)),
            pltpu.SemaphoreType.DMA((2,)),
            pltpu.SemaphoreType.DMA((2,)),
        ],
        compiler_params=pltpu.CompilerParams(collective_id=0, has_side_effects=True),
    )(state, flat, table.T, thermal.reshape(1, CLASSES), output_mode_row.reshape(1, 64))
    return pl.pallas_call(
        finish,
        out_shape=(
            jax.ShapeDtypeStruct((ROWS, 128), f32),
            jax.ShapeDtypeStruct((OWN, 1024), f32),
        ),
        in_specs=[pl.BlockSpec(memory_space=pltpu.VMEM)] * 2,
        out_specs=(anywhere,) * 2,
        scratch_shapes=[pltpu.SemaphoreType.DMA((12,))],
    )(pltpu.with_memory_space_constraint(updated, pltpu.VMEM), pltpu.with_memory_space_constraint(terms, pltpu.VMEM))


def solution(mesh):
    in_specs = (P(None, ("space", "mode")), P("mode", None, None), P(), P(), P())
    out_specs = (P(None, ("space", "mode")), P("mode", "space"))
    return jax.shard_map(
        functools.partial(shards, mesh.shape["space"]),
        mesh=mesh,
        in_specs=in_specs,
        out_specs=out_specs,
        check_vma=False,
    )
```

```python
import functools

import jax
import jax.numpy as jnp
from jax import lax
from jax.experimental import pallas as pl
from jax.experimental.pallas import tpu as pltpu
from jax.sharding import PartitionSpec as P

CLASSES = 3
MODES = 286
ROWS = CLASSES * MODES
PAD = 864
HALF = 432
OWN = 8

wave_bound = 5.2
courant = 0.09
collision_update = 0.1

MESH = pl.DeviceIdType.MESH


def kernel(
    spaces,
    state_hbm,
    tensor_hbm,
    table_hbm,
    thermal_hbm,
    target_hbm,
    updated,
    terms_out,
    state,
    tensor,
    table,
    thermal,
    target,
    slab,
    first,
    terms,
    edge_out,
    edge_in,
    matrix,
    delta,
    base,
    placing,
    load_sem,
    z_send,
    z_recv,
    c_send,
    c_recv,
    t_send,
    t_recv,
    e_send,
    e_recv,
):
    space = lax.axis_index("space")
    me = lax.axis_index("mode")
    q, c = me // 2, me % 2
    partner = me + 1 - 2 * c
    right_q, left_q, far_q = (q + 1) % 4, (q + 3) % 4, (q + 2) % 4
    right, left, far = 2 * right_q + c, 2 * left_q + c, 2 * far_q + c

    after = me + 1
    before = me + 7
    after_space = (space + after // 8) % spaces
    before_space = (space + spaces - 1 + before // 8) % spaces
    after_id = {"space": after_space, "mode": after % 8}
    before_id = {"space": before_space, "mode": before % 8}

    sideways_id = {
        "space": jnp.where(c == 0, before_id["space"], after_id["space"]),
        "mode": jnp.where(c == 0, before_id["mode"], after_id["mode"]),
    }

    barrier = pltpu.get_barrier_semaphore()
    for device in ({"mode": right}, {"mode": left}, {"mode": partner}, sideways_id):
        pl.semaphore_signal(barrier, inc=1, device_id=device, device_id_type=MESH)

    def load(source, dest, sem):
        copy = pltpu.make_async_copy(source, dest, load_sem.at[sem])
        copy.start()
        return copy

    state_loads = []
    for part in range(4):
        rows = pl.ds(216 * part, min(216, ROWS - 216 * part))
        state_loads.append(load(state_hbm.at[rows], state.at[rows], 5 + part))
    table_load = load(table_hbm, table, 2)
    thermal_load = load(thermal_hbm, thermal, 3)
    target_load = load(target_hbm, target, 4)

    def remote(source, dest, send, recv, device):
        return pltpu.make_async_remote_copy(
            src_ref=source,
            dst_ref=dest,
            send_sem=send,
            recv_sem=recv,
            device_id=device,
            device_id_type=MESH,
        )

    def half(slot, h):
        return slab.at[slot, pl.ds(pl.multiple_of(h * HALF, 16), HALF)]

    def over_z(slot, h, i, device):
        return remote(half(slot, h), half(slot, h), z_send.at[i], z_recv.at[i], {"mode": device})

    def over_chip(slot, h, i):
        return remote(half(slot, h), half(slot, h), c_send.at[i], c_recv.at[i], {"mode": partner})

    for copy in state_loads:
        copy.wait()
    tensor_load = load(tensor_hbm, tensor, 1)
    state[pl.ds(ROWS, 896 - ROWS), :] = jnp.zeros((896 - ROWS, 128), jnp.float32)
    slab[me] = state[pl.ds(0, PAD), :].astype(jnp.bfloat16)

    pl.semaphore_wait(barrier, 4)

    own = [
        over_z(me, 0, 0, right),
        over_z(me, 1, 1, left),
        over_z(me, 1, 2, right),
        over_z(me, 0, 3, left),
        over_chip(me, 0, 0),
        over_chip(me, 1, 1),
    ]
    for copy in own[4:] + own[:4]:
        copy.start()

    edge_out[...] = jnp.zeros_like(edge_out)
    for t in range(7):
        turned = jnp.transpose(state[pl.ds(128 * t, 128), :])
        edge_out[0, pl.ds(t, 1), :] = turned[0:1, :]
        edge_out[1, pl.ds(t, 1), :] = turned[127:128, :]
    edges = [
        remote(edge_out.at[0], edge_in.at[1], e_send.at[0], e_recv.at[0], before_id),
        remote(edge_out.at[1], edge_in.at[0], e_send.at[1], e_recv.at[1], after_id),
    ]
    for copy in edges:
        copy.start()

    table_load.wait()
    thermal_load.wait()
    target_load.wait()
    along = table[0:1, :]
    codes = along * 144 + table[1:2, :] * 12 + table[2:3, :]
    spread = jnp.broadcast_to(
        jnp.concatenate([codes.astype(jnp.float32), jnp.zeros((1, 384 - MODES), jnp.float32)], axis=1),
        (128, 384),
    )
    code_column = jnp.transpose(spread)[:MODES, 0:1]
    n = along.astype(jnp.float32)
    gap = code_column - codes.astype(jnp.float32)
    matrix[...] = jnp.where(gap == 144.0, jnp.sqrt(n + 1.0), 0.0) + jnp.where(
        gap == -144.0, jnp.sqrt(n), 0.0
    )
    row_index = lax.broadcasted_iota(jnp.int32, (ROWS, 128), 0)
    twice = jnp.concatenate([target[...], target[...]], axis=1)
    placing[...] = jnp.where(row_index == twice, 1.0, 0.0).astype(jnp.bfloat16)

    spot = lax.broadcasted_iota(jnp.int32, (OWN, 64), 1) - lax.broadcasted_iota(
        jnp.int32, (OWN, 64), 0
    )
    own_target = jnp.sum(
        jnp.where(spot == me * OWN, target[...].astype(jnp.float32), 0.0), axis=1, keepdims=True
    )
    wide = jnp.broadcast_to(own_target, (OWN, 256))
    in_first = wide < float(MODES)
    in_second = wide < float(2 * MODES)

    def transport():
        edges[0].wait_recv()
        edges[1].wait_recv()
        turned = jnp.transpose(
            jnp.concatenate(
                [edge_in[0], edge_in[1], jnp.zeros((112, 128), jnp.float32)], axis=0
            )
        )
        lane = lax.broadcasted_iota(jnp.int32, (128, 128), 1)
        speed = [thermal[0:1, d : d + 1] for d in range(CLASSES)]
        for t in range(7):
            x = state[pl.ds(128 * t, 128), :]
            lower = jnp.where(lane == 0, turned[:, t : t + 1], pltpu.roll(x, 1, 1))
            upper = jnp.where(lane == 127, turned[:, 8 + t : 9 + t], pltpu.roll(x, 127, 1))
            row = lax.broadcasted_iota(jnp.int32, (128, 128), 0) + 128 * t
            scale = jnp.where(
                row < MODES, speed[0], jnp.where(row < 2 * MODES, speed[1], speed[2])
            )
            delta[pl.ds(128 * t, 128), :] = (0.5 * courant) * scale * (upper - lower)
            base[pl.ds(128 * t, 128), :] = x + (0.5 * courant * wave_bound) * scale * (
                (upper - x) - (x - lower)
            )
        for d in range(CLASSES):
            rows = pl.ds(MODES * d, MODES)
            base[rows, :] = base[rows, :] - jnp.dot(
                matrix[...],
                delta[rows, :],
                precision=lax.Precision.HIGHEST,
                preferred_element_type=jnp.float32,
            )

    def give(slot):
        return remote(
            terms_out.at[slot], terms.at[me], t_send.at[slot], t_recv.at[me], {"mode": slot}
        )

    def take(other):
        return remote(
            terms_out.at[other], terms.at[other], t_send.at[other], t_recv.at[other], {"mode": other}
        )

    near = jnp.where((q == 0) | (q == 3), 1, 0)
    sides = (near, 1 - near)

    def side_chip(side):
        return jnp.where(side == 0, left_q, right_q)

    near_q, next_q = side_chip(near), side_chip(1 - near)
    order = (
        q,
        jnp.where(q == 2, far_q, near_q),
        jnp.where(q == 2, near_q, jnp.where(q == 3, far_q, next_q)),
        jnp.where(q < 2, far_q, next_q),
    )

    def pass_early(side):
        slot, back = 2 * side_chip(side) + c, 2 * side_chip(1 - side) + c
        over_z(slot, side, side, back).wait_recv()
        over_z(slot, side, 4 + side, back).start()
        over_chip(slot, side, 2 + side).start()

    def pass_late(side):
        slot, back = 2 * side_chip(side) + c, 2 * side_chip(1 - side) + c
        over_z(slot, 1 - side, 2 + side, back).wait_recv()
        over_chip(slot, 1 - side, 4 + side).start()

    def pass_far():
        for side in range(2):
            over_z(far, side, 4 + side, right).wait_recv()
            over_chip(far, side, 6 + side).start()

    def await_partner(chip):
        slot = 2 * chip + 1 - c
        low = jnp.where(chip == left_q, 2, jnp.where(chip == right_q, 5, 6))
        high = jnp.where(chip == left_q, 4, jnp.where(chip == right_q, 3, 7))
        over_chip(slot, 0, low).wait_recv()
        over_chip(slot, 1, high).wait_recv()

    def step(k, carry):
        chip = jnp.where(k == 0, order[0], jnp.where(k == 1, order[1], jnp.where(k == 2, order[2], order[3])))

        @pl.when(k == 0)
        def _():
            pass_early(0)
            pass_early(1)
            tensor_load.wait()
            over_chip(partner, 0, 0).wait_recv()
            over_chip(partner, 1, 1).wait_recv()

        @pl.when(k == 1)
        def _():
            pass_late(sides[0])
            pass_late(sides[1])

        @pl.when(k == jnp.where(q == 2, 1, 2))
        def _():
            pass_far()

        @pl.when(k > 0)
        def _():
            await_partner(chip)

        rhs = jnp.concatenate([slab[2 * chip], slab[2 * chip + 1]], axis=1)[:ROWS, :]
        first[...] = rhs.astype(jnp.float32)
        product = jnp.dot(tensor[...], rhs, preferred_element_type=jnp.float32)
        total = [jnp.zeros((OWN, 256), jnp.float32)] * 4
        for i in range(MODES):
            rows = [
                jnp.broadcast_to(first[pl.ds(i + MODES * d, 1), :], (OWN, 256))
                for d in range(CLASSES)
            ]
            chosen = jnp.where(in_first, rows[0], jnp.where(in_second, rows[1], rows[2]))
            total[i % 4] += chosen * product[OWN * i : OWN * (i + 1), :]
        total = (total[0] + total[1]) + (total[2] + total[3])
        terms_out[2 * chip] = total[:, :128]
        terms_out[2 * chip + 1] = total[:, 128:]
        give(2 * chip + 1 - c).start()

        @pl.when(k == 0)
        def _():
            terms[me] = terms_out[me]

        @pl.when(k > 0)
        def _():
            give(2 * chip + c).start()

        return carry

    lax.fori_loop(0, 4, step, 0)

    transport()

    others = [(me + v) % 8 for v in range(1, 8)]
    for other in others:
        take(other).wait_recv()
    scaled = collision_update * terms[...].reshape(64, 128)
    high = scaled.astype(jnp.bfloat16)
    low = (scaled - high.astype(jnp.float32)).astype(jnp.bfloat16)
    updated[...] = (
        base[pl.ds(0, ROWS), :]
        + jnp.dot(
            placing[...],
            jnp.concatenate([high, low], axis=0),
            preferred_element_type=jnp.float32,
        )
    )
    for copy in own + edges:
        copy.wait_send()
    for side in range(2):
        over_z(me, side, 4 + side, right).wait_send()
        for i in (2, 4, 6):
            over_chip(me, side, i + side).wait_send()
    for other in others:
        give(other).wait_send()


def finish(updated, terms, updated_hbm, collision_hbm, sems):
    copies = []
    for part in range(4):
        rows = pl.ds(216 * part, min(216, ROWS - 216 * part))
        copies.append(
            pltpu.make_async_copy(updated.at[rows], updated_hbm.at[rows], sems.at[8 + part])
        )
    for slot in range(8):
        copies.append(
            pltpu.make_async_copy(
                terms.at[slot], collision_hbm.at[:, pl.ds(128 * slot, 128)], sems.at[slot]
            )
        )
    for copy in copies:
        copy.start()
    for copy in copies:
        copy.wait()


def shards(spaces, state, tensor, table, thermal, output_mode_row):
    f32, bf16 = jnp.float32, jnp.bfloat16
    flat = jnp.transpose(tensor, (1, 0, 2)).reshape(MODES * OWN, ROWS)
    anywhere = pl.BlockSpec(memory_space=pl.ANY)
    updated, terms = pl.pallas_call(
        functools.partial(kernel, spaces),
        out_shape=(pltpu.VMEM((ROWS, 128), f32), pltpu.VMEM((8, OWN, 128), f32)),
        in_specs=[anywhere] * 5,
        scratch_shapes=[
            pltpu.VMEM((896, 128), f32),
            pltpu.VMEM((MODES * OWN, ROWS), bf16),
            pltpu.VMEM((3, MODES), jnp.int32),
            pltpu.VMEM((1, CLASSES), f32),
            pltpu.VMEM((1, 64), jnp.int32),
            pltpu.VMEM((8, PAD, 128), bf16),
            pltpu.VMEM((ROWS, 256), f32),
            pltpu.VMEM((8, OWN, 128), f32),
            pltpu.VMEM((2, 8, 128), f32),
            pltpu.VMEM((2, 8, 128), f32),
            pltpu.VMEM((MODES, MODES), f32),
            pltpu.VMEM((896, 128), f32),
            pltpu.VMEM((896, 128), f32),
            pltpu.VMEM((ROWS, 128), bf16),
            pltpu.SemaphoreType.DMA((9,)),
            pltpu.SemaphoreType.DMA((6,)),
            pltpu.SemaphoreType.DMA((6,)),
            pltpu.SemaphoreType.DMA((8,)),
            pltpu.SemaphoreType.DMA((8,)),
            pltpu.SemaphoreType.DMA((8,)),
            pltpu.SemaphoreType.DMA((8,)),
            pltpu.SemaphoreType.DMA((2,)),
            pltpu.SemaphoreType.DMA((2,)),
        ],
        compiler_params=pltpu.CompilerParams(collective_id=0, has_side_effects=True),
    )(state, flat, table.T, thermal.reshape(1, CLASSES), output_mode_row.reshape(1, 64))
    return pl.pallas_call(
        finish,
        out_shape=(
            jax.ShapeDtypeStruct((ROWS, 128), f32),
            jax.ShapeDtypeStruct((OWN, 1024), f32),
        ),
        in_specs=[pl.BlockSpec(memory_space=pltpu.VMEM)] * 2,
        out_specs=(anywhere,) * 2,
        scratch_shapes=[pltpu.SemaphoreType.DMA((12,))],
    )(pltpu.with_memory_space_constraint(updated, pltpu.VMEM), pltpu.with_memory_space_constraint(terms, pltpu.VMEM))


def solution(mesh):
    in_specs = (P(None, ("space", "mode")), P("mode", None, None), P(), P(), P())
    out_specs = (P(None, ("space", "mode")), P("mode", "space"))
    return jax.shard_map(
        functools.partial(shards, mesh.shape["space"]),
        mesh=mesh,
        in_specs=in_specs,
        out_specs=out_specs,
        check_vma=False,
    )
```
